32 devices in a mesh: ctx: 8 (over y, x, core), fsdp: 4 (over z).
Axes of the slice: x: 2, y: 2, z: 4, core: 2. Of those that a mesh axis runs over, the one named last changes fastest.
Arguments:
- inner: bfloat16 [16384, 8192], P('ctx', 'fsdp'), may hold values from -6 to 6
- proj_weight: bfloat16 [32, 8192], P(None, 'fsdp'), may hold values from -0.0625 to 0.0625
- rates: float32 [8192], P('fsdp'), may hold values from 3.0517578e-06 to 0.0333333333
- keep: float32 [16384], P('ctx'), may hold values from 0.216 to 1, as said below
- skip: float32 [8192], P('fsdp'), may hold values from 0.5 to 1.5
- upstream: bfloat16 [16384, 8192], P('ctx', 'fsdp'), may hold values from -6 to 6
Outputs:
- input_grad: bfloat16 [16384, 8192], P('ctx', 'fsdp')
- proj_grad: float32 [32, 8192], P(None, 'fsdp')
The draws below stay inside these ranges and needn't reach their ends.
Inputs may be any that keep to these rules, and one draw needn't show every extreme that they name: `keep`: factors on the tokens' decays.
All inputs are finite; a program needn't handle non-finite values.
Results may differ from the reference program's by a relative error of at most 0.0058.
Values sent between devices are 32-bit elements; how exact they have to be, the bound alone decides.
A program may use at most 128 MiB of HBM per device.

```python
import math
import jax
import jax.numpy as jnp
from jax import lax

E = 8192
N = 16
BLK = 256
SEQ = 16384


def draw_rates(key, part):
    keys = jax.random.split(jax.random.fold_in(key, 5), 3)
    slow = jnp.exp(jax.random.uniform(keys[0], (E,), minval=math.log(0.05 / SEQ), maxval=math.log(0.5 / SEQ)))
    fast = jnp.exp(jax.random.uniform(keys[1], (E,), minval=math.log(1.0 / 50.0), maxval=math.log(1.0 / 30.0)))
    picked = jax.random.randint(keys[2], (E,), 0, 2) == 0
    return jnp.where(picked, fast, slow).astype(jnp.float32)


def draw_keep(key, part):
    keys = jax.random.split(jax.random.fold_in(key, 11), 2)
    places = jax.random.randint(keys[0], (3,), 0, SEQ)
    losses = jax.random.uniform(keys[1], (3,), minval=0.6, maxval=0.8)
    positions = jnp.arange(SEQ)
    struck = positions[None, :] == places[:, None]
    return jnp.prod(jnp.where(struck, losses[:, None], 1.0), axis=0).astype(jnp.float32)


def spiked(result, stream_key, source, target, parts, factor):
    def block_of(position):
        return (jnp.arange(result.shape[position]) // (result.shape[position] // parts)).reshape((-1,) + (1,) * (result.ndim - 1 - position))

    near = jax.random.permutation(stream_key, parts)[block_of(target)]
    far = (block_of(target) + parts // 2) % parts
    return jnp.where((block_of(source) == near) | (block_of(source) == far), factor * result, result)


def levels(own_key, dims, cuts, low, largest):
    gain = 1.0
    for position, parts in cuts:
        draws = jax.random.uniform(jax.random.fold_in(jax.random.fold_in(own_key, 6), position), (parts,), jnp.float32, low / len(cuts), largest / len(cuts))
        gain = gain * jnp.repeat(jnp.exp(draws), dims[position] // parts).reshape((-1,) + (1,) * (len(dims) - 1 - position))
    return gain


def centred(key, extent, width, limit, shards=(), kind=jnp.bfloat16):
    entries = jax.random.normal(key, extent, jnp.float32) * width
    if len(shards) > 0:
        entries = levels(key, extent, shards, -0.22, 0.18) * entries
    return jnp.clip(entries, min=-limit, max=limit).astype(kind)


def heavy_noise(stream_key, dims, spread, reach, shards, heavy, kind=jnp.bfloat16):
    drawn = spread * jax.random.normal(stream_key, dims, jnp.float32)
    if shards:
        drawn = drawn * levels(stream_key, dims, shards, -0.22, 0.18)
    return jnp.clip(spiked(drawn, jax.random.fold_in(stream_key, 3), *heavy), -reach, reach).astype(kind)


def setup_inputs(seed: int = 0) -> dict:
    arg_keys = jax.random.split(jax.random.key(seed), 7)
    inner = centred(arg_keys[0], (SEQ, E), 1.0, 6.0, ((0, 8), (1, 4)))
    proj_weight = centred(arg_keys[1], (2 * N, E), E ** -0.5, 0.0625, ((1, 4),))
    rates = draw_rates(jax.random.fold_in(arg_keys[6], 71), 0)
    keep = draw_keep(jax.random.fold_in(arg_keys[6], 71), 0)
    skip = jnp.clip(0.5 + 1.0 * jax.random.uniform(arg_keys[4], (E,), jnp.float32) ** levels(arg_keys[4], (E,), ((0, 4),), -0.2, 0.2), 0.5, 1.5)
    upstream = heavy_noise(arg_keys[5], (SEQ, E), 1.0, 6.0, ((0, 8), (1, 4)), (0, 1, 8, 2.0))
    return dict(inner=inner, proj_weight=proj_weight, rates=rates, keep=keep, skip=skip, upstream=upstream)


def reference(inner, proj_weight, rates, keep, skip, upstream):
    highest = lax.Precision.HIGHEST

    def mixed(left, right):
        return jnp.dot(left, right, preferred_element_type=jnp.float32)

    def precise(left, right):
        return jnp.dot(left, right, precision=highest)
    factor = 1.0 / jnp.sqrt(jnp.float32(N))
    input_scale = jnp.sqrt(-jnp.expm1(-2.0 * rates))
    offsets = jnp.arange(1, BLK + 1).astype(jnp.float32)
    within_base = jnp.exp(-offsets[:, None] * rates[None, :])
    lower_mask = jnp.tril(jnp.ones((BLK, BLK), dtype=bool))
    coeffs = jnp.dot(inner, proj_weight.T, preferred_element_type=jnp.float32)
    coef_b = coeffs.astype(jnp.bfloat16)
    nblocks = SEQ // BLK
    blocks = (inner.reshape(nblocks, BLK, E), coef_b.reshape(nblocks, BLK, 2 * N), keep.reshape(nblocks, BLK), upstream.reshape(nblocks, BLK, E), coeffs.reshape(nblocks, BLK, 2 * N))

    def prepare(block):
        vals, coef, factors, grads, coef_wide = block
        within = within_base * jnp.cumprod(factors)[:, None]
        scaled = (input_scale[None, :] * vals.astype(jnp.float32) / within).astype(jnp.bfloat16)
        weighted = (within * grads.astype(jnp.float32)).astype(jnp.bfloat16)
        return (coef[:, :N], coef[:, N:], within, scaled, weighted)

    def forward(state, block):
        write_coef, read_coef, within, scaled, weighted = prepare(block)
        new_state = within[-1][None, :] * state + within[-1][None, :] * mixed(write_coef.T, scaled)
        return (new_state, state)

    def backward(adjoint, block):
        write_coef, read_coef, within, scaled, weighted = prepare(block)
        new_adjoint = factor * mixed(read_coef.T, weighted) + within[-1][None, :] * adjoint
        return (new_adjoint, adjoint)
    zero_state = jnp.zeros((N, E), jnp.float32)
    _, state_at = lax.scan(forward, zero_state, blocks)
    _, adjoint_at = lax.scan(backward, zero_state, blocks, reverse=True)

    def finish(accum, item):
        block, state_in, adjoint = item
        write_coef, read_coef, within, scaled, weighted = prepare(block)
        grads = block[3].astype(jnp.float32)
        coef_wide = block[4]
        carried = (within[-1][None, :] * adjoint).astype(jnp.bfloat16)
        state_b = state_in.astype(jnp.bfloat16)
        read_write = jnp.where(lower_mask, mixed(read_coef, write_coef.T), 0.0).astype(jnp.bfloat16)
        grad_cross = jnp.where(lower_mask, mixed(weighted, scaled.T), 0.0)
        scan_grad = input_scale[None, :] / within * (factor * mixed(read_write.T, weighted) + mixed(write_coef, carried))
        write_wide = coef_wide[:, :N]
        read_wide = coef_wide[:, N:]
        grad_write = factor * precise(grad_cross.T, read_wide) + mixed(scaled, carried.T)
        grad_read = factor * (mixed(weighted, state_b.T) + precise(grad_cross, write_wide))
        grad_coef = jnp.concatenate([grad_write, grad_read], axis=1)
        grad_b = grad_coef.astype(jnp.bfloat16)
        back_grad = mixed(grad_b, proj_weight)
        block_grad = (scan_grad + skip[None, :] * grads + back_grad).astype(jnp.bfloat16)
        return (accum + precise(grad_coef.T, block[0].astype(jnp.float32)), block_grad)
    accum, input_grad = lax.scan(finish, jnp.zeros((2 * N, E), jnp.float32), (blocks, state_at, adjoint_at))
    return (input_grad.reshape(SEQ, E), accum / SEQ)
```

```python
import functools

import jax
import jax.numpy as jnp
from jax import lax
from jax.experimental import pallas as pl
from jax.experimental.pallas import tpu as pltpu
from jax.sharding import PartitionSpec as P

BLK = 256
MESH = pl.DeviceIdType.MESH


def greet(axis, n):
    me = lax.axis_index(axis)
    barrier = pltpu.get_barrier_semaphore()
    for k in range(1, n):
        pl.semaphore_signal(
            barrier, inc=1, device_id={axis: lax.rem(me + k, n)}, device_id_type=MESH
        )
    pl.semaphore_wait(barrier, n - 1)
    return me


def send(axis, n, me, k, src, dst, sems):
    copy = pltpu.make_async_remote_copy(
        src_ref=src,
        dst_ref=dst,
        send_sem=sems[0].at[k - 1],
        recv_sem=sems[1].at[k - 1],
        device_id={axis: lax.rem(me + k, n)},
        device_id_type=MESH,
    )
    copy.start()
    return copy


def reduce_kernel(axis, n, x_ref, o_ref, parts, total, s1, r1, s2, r2):
    me = greet(axis, n)
    copies = [
        send(axis, n, me, k, x_ref.at[lax.rem(me + k, n)], parts.at[k - 1], (s1, r1))
        for k in range(1, n)
    ]
    acc = x_ref[me]
    for k in range(1, n):
        copies[k - 1].wait_recv()
        acc = acc + parts[k - 1]
    total[me] = acc
    back = [send(axis, n, me, k, total.at[me], total.at[me], (s2, r2)) for k in range(1, n)]
    for copy in copies:
        copy.wait_send()
    for copy in back:
        copy.wait()
    o_ref[...] = total[...]


def reduced(x, axis, ident):
    n = x.shape[0]
    vmem = pl.BlockSpec(memory_space=pltpu.VMEM)
    return pl.pallas_call(
        functools.partial(reduce_kernel, axis, n),
        out_shape=jax.ShapeDtypeStruct(x.shape, x.dtype),
        in_specs=[vmem],
        out_specs=vmem,
        scratch_shapes=[
            pltpu.VMEM((n - 1,) + x.shape[1:], x.dtype),
            pltpu.VMEM(x.shape, x.dtype),
        ]
        + [pltpu.SemaphoreType.DMA((n - 1,))] * 4,
        compiler_params=pltpu.CompilerParams(collective_id=ident, has_side_effects=True),
    )(x)


def split(x, n):
    rows, length = x.shape
    return x.reshape(rows, n, length // n).transpose(1, 0, 2)


def join(x):
    n, rows, part = x.shape
    return x.transpose(1, 0, 2).reshape(rows, n * part)


def all_reduced(x, axis, ident):
    return join(reduced(split(x, lax.axis_size(axis)), axis, ident))


def scan_kernel(axis, n, nstate, x_ref, o_ref, got, out, home, s1, r1, s2, r2):
    me = greet(axis, n)
    copies = [
        send(axis, n, me, k, x_ref.at[lax.rem(me + k, n)], got.at[me], (s1, r1))
        for k in range(1, n)
    ]
    got[me] = x_ref[me]
    for copy in copies:
        copy.wait()
    zero = jnp.zeros((nstate, x_ref.shape[2]), jnp.float32)
    state = zero
    adjoint = zero
    for k in range(n):
        out[k, :nstate] = state
        state = got[k, :nstate] + got[k, 2 * nstate : 2 * nstate + 1] * state
        j = n - 1 - k
        out[j, nstate:] = adjoint
        adjoint = got[j, nstate : 2 * nstate] + got[j, 2 * nstate : 2 * nstate + 1] * adjoint
    back = [
        send(axis, n, me, k, out.at[lax.rem(me + k, n)], home.at[me], (s2, r2))
        for k in range(1, n)
    ]
    home[me] = out[me]
    for copy in back:
        copy.wait()
    o_ref[...] = home[...]


def scanned(x, nstate, axis, ident):
    n, rows, part = x.shape
    vmem = pl.BlockSpec(memory_space=pltpu.VMEM)
    small = (n, 2 * nstate, part)
    return pl.pallas_call(
        functools.partial(scan_kernel, axis, n, nstate),
        out_shape=jax.ShapeDtypeStruct(small, x.dtype),
        in_specs=[vmem],
        out_specs=vmem,
        scratch_shapes=[
            pltpu.VMEM(x.shape, x.dtype),
            pltpu.VMEM(small, x.dtype),
            pltpu.VMEM(small, x.dtype),
        ]
        + [pltpu.SemaphoreType.DMA((n - 1,))] * 4,
        compiler_params=pltpu.CompilerParams(collective_id=ident, has_side_effects=True),
    )(x)


def batched(form, left, right):
    return jnp.einsum(form, left, right, preferred_element_type=jnp.float32)


def precise(form, left, right):
    return jnp.einsum(
        form, left, right, precision=lax.Precision.HIGHEST, preferred_element_type=jnp.float32
    )


def local(inner, proj_weight, rates, keep, skip, upstream):
    length = inner.shape[0]
    channels = inner.shape[1]
    nstate = proj_weight.shape[0] // 2
    nblocks = length // BLK
    partial_coef = lax.dot_general(
        proj_weight, inner, (((1,), (1,)), ((), ())), preferred_element_type=jnp.float32
    )
    coeffs = all_reduced(partial_coef, "fsdp", 0).T
    coef_wide = coeffs.reshape(nblocks, BLK, 2 * nstate)
    write_wide = coef_wide[:, :, :nstate]
    read_wide = coef_wide[:, :, nstate:]
    coef_blocks = coeffs.astype(jnp.bfloat16).reshape(nblocks, BLK, 2 * nstate)
    write_coef = coef_blocks[:, :, :nstate]
    read_coef = coef_blocks[:, :, nstate:]
    factor = 1.0 / jnp.sqrt(jnp.float32(nstate))
    input_scale = jnp.sqrt(-jnp.expm1(-2.0 * rates))
    offsets = jnp.arange(1, BLK + 1).astype(jnp.float32)
    within_base = jnp.exp(-offsets[:, None] * rates[None, :])
    within = within_base[None] * jnp.cumprod(keep.reshape(nblocks, BLK), axis=1)[:, :, None]
    upstream_f = upstream.astype(jnp.float32).reshape(nblocks, BLK, channels)
    scaled = (
        input_scale[None, None, :]
        * inner.astype(jnp.float32).reshape(nblocks, BLK, channels)
        / within
    ).astype(jnp.bfloat16)
    weighted = (within * upstream_f).astype(jnp.bfloat16)
    decays = within[:, -1]
    state_terms = decays[:, None, :] * batched("jbn,jbe->jne", write_coef, scaled)
    adjoint_terms = factor * batched("jbn,jbe->jne", read_coef, weighted)

    def forward(state, item):
        return (item[0][None, :] * state + item[1], state)

    def backward(adjoint, item):
        return (item[1] + item[0][None, :] * adjoint, adjoint)

    zero_state = jnp.zeros((nstate, channels), jnp.float32)
    state_end, state_local = lax.scan(forward, zero_state, (decays, state_terms))
    adjoint_start, adjoint_local = lax.scan(
        backward, zero_state, (decays, adjoint_terms), reverse=True
    )
    device_decay = jnp.prod(decays, axis=0)
    ones_row = jnp.ones((1, channels), jnp.float32)
    before = jnp.concatenate([ones_row, jnp.cumprod(decays, axis=0)[:-1]], axis=0)
    after = jnp.flip(
        jnp.concatenate([ones_row, jnp.cumprod(jnp.flip(decays, 0), axis=0)[:-1]], axis=0), 0
    )
    packed = jnp.concatenate(
        [state_end, adjoint_start, jnp.broadcast_to(device_decay[None, :], (8, channels))], axis=0
    )
    arrived = join(scanned(split(packed, lax.axis_size("ctx")), nstate, "ctx", 1))
    state_in = arrived[:nstate]
    adjoint_in = arrived[nstate:]
    state_at = (state_local + before[:, None, :] * state_in[None]).astype(jnp.bfloat16)
    adjoint_at = adjoint_local + after[:, None, :] * adjoint_in[None]
    carried = (decays[:, None, :] * adjoint_at).astype(jnp.bfloat16)
    lower_mask = jnp.tril(jnp.ones((BLK, BLK), dtype=bool))
    read_write = jnp.where(
        lower_mask[None], batched("jbn,jcn->jbc", read_coef, write_coef), 0.0
    ).astype(jnp.bfloat16)
    grad_cross = jnp.where(lower_mask[None], batched("jbe,jce->jbc", weighted, scaled), 0.0)
    scan_grad = (
        input_scale[None, None, :]
        / within
        * (
            factor * batched("jbc,jbe->jce", read_write, weighted)
            + batched("jcn,jne->jce", write_coef, carried)
        )
    )
    grad_write = factor * precise("jbc,jbn->jcn", grad_cross, read_wide) + batched(
        "jce,jne->jcn", scaled, carried
    )
    grad_read = factor * (
        batched("jbe,jne->jbn", weighted, state_at)
        + precise("jbc,jcn->jbn", grad_cross, write_wide)
    )
    partial_grad = jnp.concatenate([grad_write, grad_read], axis=2).reshape(length, 2 * nstate)
    grad_coef = all_reduced(partial_grad.T, "fsdp", 2).T
    grad_short = grad_coef.astype(jnp.bfloat16)
    back_grad = jnp.dot(grad_short, proj_weight, preferred_element_type=jnp.float32)
    input_grad = (
        scan_grad.reshape(length, channels)
        + skip[None, :] * upstream_f.reshape(length, channels)
        + back_grad
    ).astype(jnp.bfloat16)
    local_proj = lax.dot_general(
        grad_coef,
        inner.astype(jnp.float32),
        (((0,), (0,)), ((), ())),
        precision=lax.Precision.HIGHEST,
        preferred_element_type=jnp.float32,
    )
    proj_total = all_reduced(local_proj, "ctx", 3)
    return (input_grad, proj_total / (length * lax.axis_size("ctx")))


def solution(mesh):
    placed = (P("ctx", "fsdp"), P(None, "fsdp"), P("fsdp"), P("ctx"), P("fsdp"), P("ctx", "fsdp"))
    return jax.shard_map(
        local,
        mesh=mesh,
        in_specs=placed,
        out_specs=(P("ctx", "fsdp"), P(None, "fsdp")),
        check_vma=False,
    )
```

```python
import functools

import jax
import jax.numpy as jnp
from jax import lax
from jax.experimental import pallas as pl
from jax.experimental.pallas import tpu as pltpu
from jax.sharding import PartitionSpec as P

BLK = 256
MESH = pl.DeviceIdType.MESH


def greet(axis, n):
    me = lax.axis_index(axis)
    barrier = pltpu.get_barrier_semaphore()
    for k in range(1, n):
        pl.semaphore_signal(
            barrier, inc=1, device_id={axis: lax.rem(me + k, n)}, device_id_type=MESH
        )
    pl.semaphore_wait(barrier, n - 1)
    return me


def send(axis, n, me, k, src, dst, sems):
    copy = pltpu.make_async_remote_copy(
        src_ref=src,
        dst_ref=dst,
        send_sem=sems[0].at[k - 1],
        recv_sem=sems[1].at[k - 1],
        device_id={axis: lax.rem(me + k, n)},
        device_id_type=MESH,
    )
    copy.start()
    return copy


def reduce_kernel(axis, n, x_ref, o_ref, parts, total, s1, r1, s2, r2):
    me = greet(axis, n)
    copies = [
        send(axis, n, me, k, x_ref.at[lax.rem(me + k, n)], parts.at[k - 1], (s1, r1))
        for k in range(1, n)
    ]
    acc = x_ref[me]
    for k in range(1, n):
        copies[k - 1].wait_recv()
        acc = acc + parts[k - 1]
    total[me] = acc
    back = [send(axis, n, me, k, total.at[me], total.at[me], (s2, r2)) for k in range(1, n)]
    for copy in copies:
        copy.wait_send()
    for copy in back:
        copy.wait()
    o_ref[...] = total[...]


def reduced(x, axis, ident):
    n = x.shape[0]
    vmem = pl.BlockSpec(memory_space=pltpu.VMEM)
    return pl.pallas_call(
        functools.partial(reduce_kernel, axis, n),
        out_shape=jax.ShapeDtypeStruct(x.shape, x.dtype),
        in_specs=[vmem],
        out_specs=vmem,
        scratch_shapes=[
            pltpu.VMEM((n - 1,) + x.shape[1:], x.dtype),
            pltpu.VMEM(x.shape, x.dtype),
        ]
        + [pltpu.SemaphoreType.DMA((n - 1,))] * 4,
        compiler_params=pltpu.CompilerParams(collective_id=ident, has_side_effects=True),
    )(x)


def split(x, n):
    rows, length = x.shape
    return x.reshape(rows, n, length // n).transpose(1, 0, 2)


def join(x):
    n, rows, part = x.shape
    return x.transpose(1, 0, 2).reshape(rows, n * part)


def all_reduced(x, axis, ident):
    return join(reduced(split(x, lax.axis_size(axis)), axis, ident))


def scan_kernel(axis, n, nstate, x_ref, o_ref, got, out, home, s1, r1, s2, r2):
    me = greet(axis, n)
    copies = [
        send(axis, n, me, k, x_ref.at[lax.rem(me + k, n)], got.at[me], (s1, r1))
        for k in range(1, n)
    ]
    got[me] = x_ref[me]
    for copy in copies:
        copy.wait()
    zero = jnp.zeros((nstate, x_ref.shape[2]), jnp.float32)
    state = zero
    adjoint = zero
    for k in range(n):
        out[k, :nstate] = state
        state = got[k, :nstate] + got[k, 2 * nstate : 2 * nstate + 1] * state
        j = n - 1 - k
        out[j, nstate:] = adjoint
        adjoint = got[j, nstate : 2 * nstate] + got[j, 2 * nstate : 2 * nstate + 1] * adjoint
    back = [
        send(axis, n, me, k, out.at[lax.rem(me + k, n)], home.at[me], (s2, r2))
        for k in range(1, n)
    ]
    home[me] = out[me]
    for copy in back:
        copy.wait()
    o_ref[...] = home[...]


def scanned(x, nstate, axis, ident):
    n, rows, part = x.shape
    vmem = pl.BlockSpec(memory_space=pltpu.VMEM)
    small = (n, 2 * nstate, part)
    return pl.pallas_call(
        functools.partial(scan_kernel, axis, n, nstate),
        out_shape=jax.ShapeDtypeStruct(small, x.dtype),
        in_specs=[vmem],
        out_specs=vmem,
        scratch_shapes=[
            pltpu.VMEM(x.shape, x.dtype),
            pltpu.VMEM(small, x.dtype),
            pltpu.VMEM(small, x.dtype),
        ]
        + [pltpu.SemaphoreType.DMA((n - 1,))] * 4,
        compiler_params=pltpu.CompilerParams(collective_id=ident, has_side_effects=True),
    )(x)


def nt(left, right, **how):
    return lax.dot_general(
        left, right, (((1,), (1,)), ((), ())), preferred_element_type=jnp.float32, **how
    )


def tn(left, right):
    return lax.dot_general(
        left, right, (((0,), (0,)), ((), ())), preferred_element_type=jnp.float32
    )


def nn(left, right, **how):
    return jnp.dot(left, right, preferred_element_type=jnp.float32, **how)


def fill(rates_ref, scale_ref, base, inverse):
    offsets = lax.broadcasted_iota(jnp.int32, base.shape, 0).astype(jnp.float32) + 1.0
    base[...] = jnp.exp(-offsets * rates_ref[...])
    inverse[...] = scale_ref[...] / base[...]


def pieces(channels):
    width = 512 if channels % 512 == 0 else channels
    return [slice(at, at + width) for at in range(0, channels, width)]


def scaled_of(inner_ref, inverse, reach, cols):
    return (inner_ref[:, cols].astype(jnp.float32) * inverse[:, cols] * (1.0 / reach)).astype(jnp.bfloat16)


def weighted_of(upstream_ref, base, reach, cols):
    return (upstream_ref[:, cols].astype(jnp.float32) * (base[:, cols] * reach)).astype(jnp.bfloat16)


def lower():
    row = lax.broadcasted_iota(jnp.int32, (BLK, BLK), 0)
    col = lax.broadcasted_iota(jnp.int32, (BLK, BLK), 1)
    return row >= col


def cross_kernel(
    nstate, factor, inner, upstream, coef, reach_ref, rates, scale,
    cross, states, before, terms, pack, base, inverse,
):
    @pl.when(pl.program_id(0) == 0)
    def _():
        fill(rates, scale, base, inverse)
        pack[: 2 * nstate] = jnp.zeros_like(pack[: 2 * nstate])
        pack[2 * nstate :] = jnp.ones_like(pack[2 * nstate :])

    reach = reach_ref[...]
    short = coef[...].astype(jnp.bfloat16)
    write, read = short[:nstate], short[nstate:]
    total = jnp.zeros((BLK, BLK), jnp.float32)
    for cols in pieces(inner.shape[1]):
        scaled = scaled_of(inner, inverse, reach, cols)
        weighted = weighted_of(upstream, base, reach, cols)
        total = total + nt(weighted, scaled)
        decay = base[BLK - 1 :, cols] * reach[BLK - 1 :]
        state = pack[:nstate, cols]
        sofar = pack[2 * nstate :, cols]
        term = factor * nn(read, weighted)
        states[0, :, cols] = state
        before[0, :, cols] = sofar[:1]
        terms[0, :, cols] = term
        pack[:nstate, cols] = decay * state + decay * nn(write, scaled)
        pack[nstate : 2 * nstate, cols] = pack[nstate : 2 * nstate, cols] + sofar[:1] * term
        pack[2 * nstate :, cols] = sofar * decay
    cross[0] = jnp.where(lower(), total, 0.0)


def grad_kernel(
    nstate, factor, inner, upstream, coef, reach_ref, rates, scale,
    cross, states, before, terms, arrived, grad, carried_ref, base, inverse, adjoint,
):
    @pl.when(pl.program_id(0) == 0)
    def _():
        fill(rates, scale, base, inverse)
        adjoint[...] = arrived[nstate:]

    reach = reach_ref[...]
    exact = dict(precision=lax.Precision.HIGHEST)
    write_part = jnp.zeros((nstate, BLK), jnp.float32)
    read_part = jnp.zeros((nstate, BLK), jnp.float32)
    for cols in pieces(inner.shape[1]):
        scaled = scaled_of(inner, inverse, reach, cols)
        weighted = weighted_of(upstream, base, reach, cols)
        decay = base[BLK - 1 :, cols] * reach[BLK - 1 :]
        later = decay * adjoint[:, cols]
        carried = later.astype(jnp.bfloat16)
        adjoint[:, cols] = terms[0, :, cols] + later
        carried_ref[0, :, cols] = carried
        state = (states[0, :, cols] + before[0, :, cols] * arrived[:nstate, cols]).astype(jnp.bfloat16)
        write_part = write_part + nt(carried, scaled)
        read_part = read_part + nt(state, weighted)
    grad[:nstate] = factor * nn(coef[nstate:], cross[0], **exact) + write_part
    grad[nstate:] = factor * (read_part + nt(coef[:nstate], cross[0], **exact))


def final_kernel(
    nstate, factor, inner, upstream, coef, reach_ref, rates, scale,
    carried, grad, weight, skip, out, proj, base, inverse,
):
    @pl.when(pl.program_id(0) == 0)
    def _():
        fill(rates, scale, base, inverse)
        proj[...] = jnp.zeros_like(proj)

    reach = reach_ref[...]
    short = coef[...].astype(jnp.bfloat16)
    write, read = short[:nstate], short[nstate:]
    row = lax.broadcasted_iota(jnp.int32, (BLK, BLK), 0)
    col = lax.broadcasted_iota(jnp.int32, (BLK, BLK), 1)
    turned = jnp.where(col >= row, tn(write, read), 0.0).astype(jnp.bfloat16)
    full = grad[...]
    high = full.astype(jnp.bfloat16)
    rest = full - high.astype(jnp.float32)
    middle = rest.astype(jnp.bfloat16)
    low = (rest - middle.astype(jnp.float32)).astype(jnp.bfloat16)
    stack = jnp.concatenate([high, middle, low], axis=0)
    size = 2 * nstate
    for cols in pieces(inner.shape[1]):
        weighted = weighted_of(upstream, base, reach, cols)
        mixed = factor * nn(turned, weighted) + tn(write, carried[0, :, cols])
        value = inverse[:, cols] * (1.0 / reach) * mixed
        value = value + skip[:, cols] * upstream[:, cols].astype(jnp.float32)
        value = value + tn(high, weight[:, cols])
        out[:, cols] = value.astype(jnp.bfloat16)
        three = nn(stack, inner[:, cols])
        proj[:, cols] = proj[:, cols] + (three[:size] + (three[size : 2 * size] + three[2 * size :]))


def local(inner, proj_weight, rates, keep, skip, upstream):
    length, channels = inner.shape
    nstate = proj_weight.shape[0] // 2
    size = 2 * nstate
    nblocks = length // BLK
    f32 = jnp.float32
    partial_coef = nt(proj_weight, inner)
    coef = all_reduced(partial_coef, "fsdp", 0)
    factor = 1.0 / nstate**0.5
    scale = jnp.sqrt(-jnp.expm1(-2.0 * rates))[None]
    rates = rates[None]
    reach = jnp.cumprod(keep.reshape(nblocks, BLK), axis=1).reshape(length, 1)
    params = pltpu.CompilerParams(
        dimension_semantics=("arbitrary",), vmem_limit_bytes=48 * 2**20
    )

    def specs(turn):
        tokens = pl.BlockSpec((BLK, channels), lambda i: (turn(i), 0))
        coefs = pl.BlockSpec((size, BLK), lambda i: (0, turn(i)))
        column = pl.BlockSpec((BLK, 1), lambda i: (turn(i), 0))
        line = pl.BlockSpec((1, channels), lambda i: (0, 0))
        return tokens, coefs, column, line

    def per_block(turn, rows, width):
        return pl.BlockSpec((1, rows, width), lambda i: (turn(i), 0, 0))

    def whole(rows):
        return pl.BlockSpec((rows, channels), lambda i: (0, 0))

    def up(i):
        return i

    def down(i):
        return nblocks - 1 - i

    tables = [pltpu.VMEM((BLK, channels), f32)] * 2
    tokens, coefs, column, line = specs(up)
    shape = jax.ShapeDtypeStruct
    cross, states, before, terms, pack = pl.pallas_call(
        functools.partial(cross_kernel, nstate, factor),
        grid=(nblocks,),
        in_specs=[tokens, tokens, coefs, column, line, line],
        out_specs=[
            per_block(up, BLK, BLK),
            per_block(up, nstate, channels),
            per_block(up, 1, channels),
            per_block(up, nstate, channels),
            whole(size + 8),
        ],
        out_shape=[
            shape((nblocks, BLK, BLK), f32),
            shape((nblocks, nstate, channels), f32),
            shape((nblocks, 1, channels), f32),
            shape((nblocks, nstate, channels), f32),
            shape((size + 8, channels), f32),
        ],
        scratch_shapes=tables,
        compiler_params=params,
    )(inner, upstream, coef, reach, rates, scale)
    arrived = join(scanned(split(pack, lax.axis_size("ctx")), nstate, "ctx", 1))
    back_tokens, back_coefs, back_column, _ = specs(down)
    partial_grad, carried = pl.pallas_call(
        functools.partial(grad_kernel, nstate, factor),
        grid=(nblocks,),
        in_specs=[back_tokens, back_tokens, back_coefs, back_column, line, line]
        + [
            per_block(down, BLK, BLK),
            per_block(down, nstate, channels),
            per_block(down, 1, channels),
            per_block(down, nstate, channels),
            whole(size),
        ],
        out_specs=[back_coefs, per_block(down, nstate, channels)],
        out_shape=[
            shape((size, length), f32),
            shape((nblocks, nstate, channels), jnp.bfloat16),
        ],
        scratch_shapes=tables + [pltpu.VMEM((nstate, channels), f32)],
        compiler_params=params,
    )(inner, upstream, coef, reach, rates, scale, cross, states, before, terms, arrived)
    grad = all_reduced(partial_grad, "fsdp", 2)
    input_grad, proj = pl.pallas_call(
        functools.partial(final_kernel, nstate, factor),
        grid=(nblocks,),
        in_specs=[tokens, tokens, coefs, column, line, line]
        + [per_block(up, nstate, channels), coefs, whole(size), line],
        out_specs=[tokens, whole(size)],
        out_shape=[shape((length, channels), jnp.bfloat16), shape((size, channels), f32)],
        scratch_shapes=tables,
        compiler_params=params,
    )(inner, upstream, coef, reach, rates, scale, carried, grad, proj_weight, skip[None])
    total = all_reduced(proj, "ctx", 3)
    return (input_grad, total / (length * lax.axis_size("ctx")))


def solution(mesh):
    placed = (P("ctx", "fsdp"), P(None, "fsdp"), P("fsdp"), P("ctx"), P("fsdp"), P("ctx", "fsdp"))
    return jax.shard_map(
        local,
        mesh=mesh,
        in_specs=placed,
        out_specs=(P("ctx", "fsdp"), P(None, "fsdp")),
        check_vma=False,
    )
```

```python
import functools

import jax
import jax.numpy as jnp
from jax import lax
from jax.experimental import pallas as pl
from jax.experimental.pallas import tpu as pltpu
from jax.sharding import PartitionSpec as P

BLK = 256
MESH = pl.DeviceIdType.MESH


def greet(axis, n):
    me = lax.axis_index(axis)
    barrier = pltpu.get_barrier_semaphore()
    for k in range(1, n):
        pl.semaphore_signal(
            barrier, inc=1, device_id={axis: lax.rem(me + k, n)}, device_id_type=MESH
        )
    pl.semaphore_wait(barrier, n - 1)
    return me


def send(axis, n, me, k, src, dst, sems):
    copy = pltpu.make_async_remote_copy(
        src_ref=src,
        dst_ref=dst,
        send_sem=sems[0].at[k - 1],
        recv_sem=sems[1].at[k - 1],
        device_id={axis: lax.rem(me + k, n)},
        device_id_type=MESH,
    )
    copy.start()
    return copy


def reduce_kernel(axis, n, x_ref, o_ref, parts, total, s1, r1, s2, r2):
    me = greet(axis, n)
    copies = [
        send(axis, n, me, k, x_ref.at[lax.rem(me + k, n)], parts.at[k - 1], (s1, r1))
        for k in range(1, n)
    ]
    acc = x_ref[me]
    for k in range(1, n):
        copies[k - 1].wait_recv()
        acc = acc + parts[k - 1]
    total[me] = acc
    back = [send(axis, n, me, k, total.at[me], total.at[me], (s2, r2)) for k in range(1, n)]
    for copy in copies:
        copy.wait_send()
    for copy in back:
        copy.wait()
    o_ref[...] = total[...]


def reduced(x, axis, ident):
    n = x.shape[0]
    vmem = pl.BlockSpec(memory_space=pltpu.VMEM)
    return pl.pallas_call(
        functools.partial(reduce_kernel, axis, n),
        out_shape=jax.ShapeDtypeStruct(x.shape, x.dtype),
        in_specs=[vmem],
        out_specs=vmem,
        scratch_shapes=[
            pltpu.VMEM((n - 1,) + x.shape[1:], x.dtype),
            pltpu.VMEM(x.shape, x.dtype),
        ]
        + [pltpu.SemaphoreType.DMA((n - 1,))] * 4,
        compiler_params=pltpu.CompilerParams(collective_id=ident, has_side_effects=True),
    )(x)


def split(x, n):
    rows, length = x.shape
    return x.reshape(rows, n, length // n).transpose(1, 0, 2)


def join(x):
    n, rows, part = x.shape
    return x.transpose(1, 0, 2).reshape(rows, n * part)


def all_reduced(x, axis, ident):
    return join(reduced(split(x, lax.axis_size(axis)), axis, ident))


def nt(left, right, **how):
    return lax.dot_general(
        left, right, (((1,), (1,)), ((), ())), preferred_element_type=jnp.float32, **how
    )


def tn(left, right):
    return lax.dot_general(
        left, right, (((0,), (0,)), ((), ())), preferred_element_type=jnp.float32
    )


def nn(left, right, **how):
    return jnp.dot(left, right, preferred_element_type=jnp.float32, **how)


def fill(rates_ref, scale_ref, base, inverse):
    offsets = lax.broadcasted_iota(jnp.int32, base.shape, 0).astype(jnp.float32) + 1.0
    base[...] = jnp.exp(-offsets * rates_ref[...])
    inverse[...] = scale_ref[...] / base[...]


def pieces(channels):
    width = 512 if channels % 512 == 0 else channels
    return [slice(at, at + width) for at in range(0, channels, width)]


def scaled_of(inner_ref, inverse, reach, cols):
    return (inner_ref[:, cols].astype(jnp.float32) * inverse[:, cols] * (1.0 / reach)).astype(jnp.bfloat16)


def weighted_of(upstream_ref, base, reach, cols):
    return (upstream_ref[:, cols].astype(jnp.float32) * (base[:, cols] * reach)).astype(jnp.bfloat16)


def lower():
    row = lax.broadcasted_iota(jnp.int32, (BLK, BLK), 0)
    col = lax.broadcasted_iota(jnp.int32, (BLK, BLK), 1)
    return row >= col


def copy_to(axis, n, me, k, src, dst, sems):
    return pltpu.make_async_remote_copy(
        src_ref=src,
        dst_ref=dst,
        send_sem=sems[0].at[k - 1],
        recv_sem=sems[1].at[k - 1],
        device_id={axis: lax.rem(me + k, n)},
        device_id_type=MESH,
    )


def scatters(n, me, part, got, sems):
    per = part.shape[0] // n
    return [
        copy_to(
            "fsdp", n, me, k, part.at[pl.ds(lax.rem(me + k, n) * per, per)], got.at[k - 1], sems
        )
        for k in range(1, n)
    ]


def gathers(n, me, total, sems):
    per = total.shape[0] // n
    own = total.at[pl.ds(me * per, per)]
    return [copy_to("fsdp", n, me, k, own, own, sems) for k in range(1, n)]


def summed(n, me, part, got, total, sems):
    per = part.shape[0] // n
    acc = part[pl.ds(me * per, per)]
    for k, copy in enumerate(scatters(n, me, part, got, sems)):
        copy.wait()
        acc = acc + got[k]
    total[pl.ds(me * per, per)] = acc


def main_kernel(
    nstate, factor, nblocks, nf, nc,
    inner, upstream, weight, reach_ref, rates, scale,
    coef_out, grad_out, carried_ref,
    base, inverse, scaled_all, weighted_all, cross, part, got, coef, gpart, ggot, grad,
    states, before, terms, pack, packed, arriving, leaving, home, arrived, adjoint,
    s1, r1, s2, r2, s3, r3, s4, r4, s5, r5, s6, r6,
):
    step = pl.program_id(0)
    size = 2 * nstate
    channels = inner.shape[1]
    width = channels // nc
    f = lax.axis_index("fsdp")
    c = lax.axis_index("ctx")
    barrier = pltpu.get_barrier_semaphore()

    @pl.when(step == 0)
    def _():
        for axis, n, me in (("fsdp", nf, f), ("ctx", nc, c)):
            for k in range(1, n):
                pl.semaphore_signal(
                    barrier, inc=1, device_id={axis: lax.rem(me + k, n)}, device_id_type=MESH
                )
        fill(rates, scale, base, inverse)
        pack[:size] = jnp.zeros_like(pack[:size])
        pack[size:] = jnp.ones_like(pack[size:])

    @pl.when(step < nblocks)
    def _():
        part[step] = nt(weight[...], inner[...])
        for cols in pieces(channels):
            scaled_all[step, :, cols] = scaled_of(inner, inverse, reach_ref[step], cols)

    @pl.when(step == nblocks)
    def _():
        pl.semaphore_wait(barrier, nf + nc - 2)
        for copy in scatters(nf, f, part, got, (s1, r1)):
            copy.start()

    @pl.when(step == nblocks + nblocks // 2)
    def _():
        summed(nf, f, part, got, coef, (s1, r1))
        for copy in gathers(nf, f, coef, (s2, r2)):
            copy.start()

    @pl.when(step >= nblocks)
    def _():
        j = step - nblocks
        total = jnp.zeros((BLK, BLK), jnp.float32)
        for cols in pieces(channels):
            weighted = weighted_of(upstream, base, reach_ref[j], cols)
            weighted_all[j, :, cols] = weighted
            total = total + nt(weighted, scaled_all[j, :, cols])
        cross[j] = jnp.where(lower(), total, 0.0)

    @pl.when(step == 2 * nblocks - 1)
    def _():
        for copy in gathers(nf, f, coef, (s2, r2)):
            copy.wait()

        def local_states(j, carry):
            short = coef[j].astype(jnp.bfloat16)
            write, read = short[:nstate], short[nstate:]
            for cols in pieces(channels):
                decay = base[BLK - 1 :, cols] * reach_ref[j, BLK - 1 :]
                state = pack[:nstate, cols]
                sofar = pack[size:, cols]
                term = factor * nn(read, weighted_all[j, :, cols])
                states[j, :, cols] = state
                before[j, :, cols] = sofar[:1]
                terms[j, :, cols] = term
                pack[:nstate, cols] = decay * state + decay * nn(write, scaled_all[j, :, cols])
                pack[nstate:size, cols] = pack[nstate:size, cols] + sofar[:1] * term
                pack[size:, cols] = sofar * decay
            return carry

        lax.fori_loop(0, nblocks, local_states, 0)
        for d in range(nc):
            packed[d] = pack[:, d * width : (d + 1) * width]
        out = [
            copy_to("ctx", nc, c, k, packed.at[lax.rem(c + k, nc)], arriving.at[c], (s3, r3))
            for k in range(1, nc)
        ]
        for copy in out:
            copy.start()
        arriving[c] = packed[c]
        for copy in out:
            copy.wait()
        state = jnp.zeros((nstate, width), jnp.float32)
        later = state
        for k in range(nc):
            leaving[k, :nstate] = state
            state = arriving[k, :nstate] + arriving[k, size : size + 1] * state
            j = nc - 1 - k
            leaving[j, nstate:] = later
            later = arriving[j, nstate:size] + arriving[j, size : size + 1] * later
        back = [
            copy_to("ctx", nc, c, k, leaving.at[lax.rem(c + k, nc)], home.at[c], (s4, r4))
            for k in range(1, nc)
        ]
        for copy in back:
            copy.start()
        home[c] = leaving[c]
        for copy in back:
            copy.wait()
        for d in range(nc):
            arrived[:, d * width : (d + 1) * width] = home[d]
        adjoint[...] = arrived[nstate:]
        exact = dict(precision=lax.Precision.HIGHEST)

        def local_grads(k, carry):
            j = nblocks - 1 - k
            write_part = jnp.zeros((nstate, BLK), jnp.float32)
            read_part = jnp.zeros((nstate, BLK), jnp.float32)
            for cols in pieces(channels):
                decay = base[BLK - 1 :, cols] * reach_ref[j, BLK - 1 :]
                later = decay * adjoint[:, cols]
                carried = later.astype(jnp.bfloat16)
                adjoint[:, cols] = terms[j, :, cols] + later
                carried_ref[j, :, cols] = carried
                state = states[j, :, cols] + before[j, :, cols] * arrived[:nstate, cols]
                write_part = write_part + nt(carried, scaled_all[j, :, cols])
                read_part = read_part + nt(state.astype(jnp.bfloat16), weighted_all[j, :, cols])
            wide = coef[j]
            gpart[j, :nstate] = factor * nn(wide[nstate:], cross[j], **exact) + write_part
            gpart[j, nstate:] = factor * (read_part + nt(wide[:nstate], cross[j], **exact))
            return carry

        lax.fori_loop(0, nblocks, local_grads, 0)
        for copy in scatters(nf, f, gpart, ggot, (s5, r5)):
            copy.start()
        coef_out[...] = coef[...]
        summed(nf, f, gpart, ggot, grad, (s5, r5))
        final = gathers(nf, f, grad, (s6, r6))
        for copy in final:
            copy.start()
        for copy in final:
            copy.wait()
        grad_out[...] = grad[...]


def final_kernel(
    nstate, factor, inner, upstream, coef, reach_ref, rates, scale,
    carried, grad, weight, skip, out, proj, base, inverse,
):
    @pl.when(pl.program_id(0) == 0)
    def _():
        fill(rates, scale, base, inverse)
        proj[...] = jnp.zeros_like(proj)

    reach = reach_ref[...]
    short = coef[0].astype(jnp.bfloat16)
    write, read = short[:nstate], short[nstate:]
    row = lax.broadcasted_iota(jnp.int32, (BLK, BLK), 0)
    col = lax.broadcasted_iota(jnp.int32, (BLK, BLK), 1)
    turned = jnp.where(col >= row, tn(write, read), 0.0).astype(jnp.bfloat16)
    full = grad[0]
    high = full.astype(jnp.bfloat16)
    rest = full - high.astype(jnp.float32)
    middle = rest.astype(jnp.bfloat16)
    low = (rest - middle.astype(jnp.float32)).astype(jnp.bfloat16)
    stack = jnp.concatenate([high, middle, low], axis=0)
    size = 2 * nstate
    for cols in pieces(inner.shape[1]):
        weighted = weighted_of(upstream, base, reach, cols)
        mixed = factor * nn(turned, weighted) + tn(write, carried[0, :, cols])
        value = inverse[:, cols] * (1.0 / reach) * mixed
        value = value + skip[:, cols] * upstream[:, cols].astype(jnp.float32)
        value = value + tn(high, weight[:, cols])
        out[:, cols] = value.astype(jnp.bfloat16)
        three = nn(stack, inner[:, cols])
        proj[:, cols] = proj[:, cols] + (three[:size] + (three[size : 2 * size] + three[2 * size :]))


def local(inner, proj_weight, rates, keep, skip, upstream):
    length, channels = inner.shape
    nstate = proj_weight.shape[0] // 2
    size = 2 * nstate
    nblocks = length // BLK
    f32 = jnp.float32
    factor = 1.0 / nstate**0.5
    scale = jnp.sqrt(-jnp.expm1(-2.0 * rates))[None]
    rates = rates[None]
    reach = jnp.cumprod(keep.reshape(nblocks, BLK), axis=1).reshape(length, 1)
    params = pltpu.CompilerParams(
        dimension_semantics=("arbitrary",), vmem_limit_bytes=48 * 2**20
    )

    nf, nc = lax.axis_size("fsdp"), lax.axis_size("ctx")
    bf16 = jnp.bfloat16
    whole = pl.BlockSpec(memory_space=pltpu.VMEM)
    shape = jax.ShapeDtypeStruct
    tables = [pltpu.VMEM((BLK, channels), f32)] * 2
    coefs = (nblocks, size, BLK)
    got = pltpu.VMEM((nf - 1, nblocks // nf, size, BLK), f32)
    entry = (nblocks, nstate, channels)
    width = channels // nc
    scratch = (
        tables
        + [pltpu.VMEM((nblocks, BLK, channels), bf16)] * 2
        + [pltpu.VMEM((nblocks, BLK, BLK), f32)]
        + [pltpu.VMEM(coefs, f32), got, pltpu.VMEM(coefs, f32)] * 2
        + [pltpu.VMEM(entry, f32), pltpu.VMEM((nblocks, 1, channels), f32), pltpu.VMEM(entry, f32)]
        + [pltpu.VMEM((size + 8, channels), f32)]
        + [pltpu.VMEM((nc, size + 8, width), f32)] * 2
        + [pltpu.VMEM((nc, size, width), f32)] * 2
        + [pltpu.VMEM((size, channels), f32), pltpu.VMEM((nstate, channels), f32)]
        + [pltpu.SemaphoreType.DMA((nf - 1,))] * 4
        + [pltpu.SemaphoreType.DMA((nc - 1,))] * 4
        + [pltpu.SemaphoreType.DMA((nf - 1,))] * 4
    )
    coef, grad, carried = pl.pallas_call(
        functools.partial(main_kernel, nstate, factor, nblocks, nf, nc),
        grid=(2 * nblocks,),
        in_specs=[
            pl.BlockSpec((BLK, channels), lambda i: (jnp.minimum(i, nblocks - 1), 0)),
            pl.BlockSpec((BLK, channels), lambda i: (jnp.maximum(i - nblocks, 0), 0)),
            whole, whole, whole, whole,
        ],
        out_specs=[whole, whole, whole],
        out_shape=[shape(coefs, f32), shape(coefs, f32), shape(entry, bf16)],
        scratch_shapes=scratch,
        compiler_params=pltpu.CompilerParams(
            dimension_semantics=("arbitrary",),
            vmem_limit_bytes=56 * 2**20,
            collective_id=0,
            has_side_effects=True,
        ),
    )(inner, upstream, proj_weight, reach.reshape(nblocks, BLK, 1), rates, scale)

    tokens = pl.BlockSpec((BLK, channels), lambda i: (i, 0))
    column = pl.BlockSpec((BLK, 1), lambda i: (i, 0))
    line = pl.BlockSpec((1, channels), lambda i: (0, 0))
    fixed = pl.BlockSpec((size, channels), lambda i: (0, 0))
    block_coef = pl.BlockSpec((1, size, BLK), lambda i: (i, 0, 0))
    block_state = pl.BlockSpec((1, nstate, channels), lambda i: (i, 0, 0))
    input_grad, proj = pl.pallas_call(
        functools.partial(final_kernel, nstate, factor),
        grid=(nblocks,),
        in_specs=[tokens, tokens, block_coef, column, line, line]
        + [block_state, block_coef, fixed, line],
        out_specs=[tokens, fixed],
        out_shape=[shape((length, channels), bf16), shape((size, channels), f32)],
        scratch_shapes=tables,
        compiler_params=params,
    )(inner, upstream, coef, reach, rates, scale, carried, grad, proj_weight, skip[None])
    total = all_reduced(proj, "ctx", 1)
    return (input_grad, total / (length * nc))


def solution(mesh):
    placed = (P("ctx", "fsdp"), P(None, "fsdp"), P("fsdp"), P("ctx"), P("fsdp"), P("ctx", "fsdp"))
    return jax.shard_map(
        local,
        mesh=mesh,
        in_specs=placed,
        out_specs=(P("ctx", "fsdp"), P(None, "fsdp")),
        check_vma=False,
    )
```

```python
import functools

import jax
import jax.numpy as jnp
from jax import lax
from jax.experimental import pallas as pl
from jax.experimental.pallas import tpu as pltpu
from jax.sharding import PartitionSpec as P

BLK = 256
MESH = pl.DeviceIdType.MESH


def nt(left, right, **how):
    return lax.dot_general(
        left, right, (((1,), (1,)), ((), ())), preferred_element_type=jnp.float32, **how
    )


def tn(left, right):
    return lax.dot_general(
        left, right, (((0,), (0,)), ((), ())), preferred_element_type=jnp.float32
    )


def nn(left, right, **how):
    return jnp.dot(left, right, preferred_element_type=jnp.float32, **how)


def fill(rates_ref, scale_ref, base, inverse):
    offsets = lax.broadcasted_iota(jnp.int32, base.shape, 0).astype(jnp.float32) + 1.0
    base[...] = jnp.exp(-offsets * rates_ref[...])
    inverse[...] = scale_ref[...] / base[...]


def pieces(channels):
    width = 512 if channels % 512 == 0 else channels
    return [slice(at, at + width) for at in range(0, channels, width)]


def scaled_of(inner_ref, inverse, reach, cols):
    return (inner_ref[:, cols].astype(jnp.float32) * inverse[:, cols] * (1.0 / reach)).astype(jnp.bfloat16)


def weighted_of(upstream_ref, base, reach, cols):
    return (upstream_ref[:, cols].astype(jnp.float32) * (base[:, cols] * reach)).astype(jnp.bfloat16)


def lower():
    row = lax.broadcasted_iota(jnp.int32, (BLK, BLK), 0)
    col = lax.broadcasted_iota(jnp.int32, (BLK, BLK), 1)
    return row >= col


def copy_to(axis, n, me, k, src, dst, sems):
    return pltpu.make_async_remote_copy(
        src_ref=src,
        dst_ref=dst,
        send_sem=sems[0].at[k - 1],
        recv_sem=sems[1].at[k - 1],
        device_id={axis: lax.rem(me + k, n)},
        device_id_type=MESH,
    )


def scatters(axis, n, me, part, got, sems):
    per = part.shape[0] // n
    return [
        copy_to(
            axis, n, me, k, part.at[pl.ds(lax.rem(me + k, n) * per, per)], got.at[k - 1], sems
        )
        for k in range(1, n)
    ]


def gathers(axis, n, me, total, sems):
    per = total.shape[0] // n
    own = total.at[pl.ds(me * per, per)]
    return [copy_to(axis, n, me, k, own, own, sems) for k in range(1, n)]


def summed(axis, n, me, part, got, total, sems):
    per = part.shape[0] // n
    acc = part[pl.ds(me * per, per)]
    for k, copy in enumerate(scatters(axis, n, me, part, got, sems)):
        copy.wait()
        acc = acc + got[k]
    total[pl.ds(me * per, per)] = acc


def main_kernel(
    nstate, factor, nblocks, nf, nc,
    inner, upstream, weight, reach_ref, rates, scale, skip,
    out, proj_out,
    base, inverse, scaled_all, weighted_all, cross, part, got, coef, gpart, ggot, grad,
    states, before, terms, pack, packed, arriving, leaving, home, arrived, adjoint,
    carried_ref, proj, ppart, pgot, ptotal,
    s1, r1, s2, r2, s3, r3, s4, r4, s5, r5, s6, r6, s7, r7, s8, r8,
):
    step = pl.program_id(0)
    size = 2 * nstate
    channels = inner.shape[1]
    width = channels // nc
    f = lax.axis_index("fsdp")
    c = lax.axis_index("ctx")
    barrier = pltpu.get_barrier_semaphore()

    @pl.when(step == 0)
    def _():
        for axis, n, me in (("fsdp", nf, f), ("ctx", nc, c)):
            for k in range(1, n):
                pl.semaphore_signal(
                    barrier, inc=1, device_id={axis: lax.rem(me + k, n)}, device_id_type=MESH
                )
        fill(rates, scale, base, inverse)
        pack[:size] = jnp.zeros_like(pack[:size])
        pack[size:] = jnp.ones_like(pack[size:])

    @pl.when(step < nblocks)
    def _():
        part[step] = nt(weight[...], inner[...])
        for cols in pieces(channels):
            scaled_all[step, :, cols] = scaled_of(inner, inverse, reach_ref[step], cols)

    @pl.when(step == nblocks)
    def _():
        pl.semaphore_wait(barrier, nf + nc - 2)
        for copy in scatters("fsdp", nf, f, part, got, (s1, r1)):
            copy.start()

    @pl.when(step == nblocks + nblocks // 2)
    def _():
        summed("fsdp", nf, f, part, got, coef, (s1, r1))
        for copy in gathers("fsdp", nf, f, coef, (s2, r2)):
            copy.start()

    @pl.when((step >= nblocks) & (step < 2 * nblocks))
    def _():
        j = step - nblocks
        total = jnp.zeros((BLK, BLK), jnp.float32)
        for cols in pieces(channels):
            weighted = weighted_of(upstream, base, reach_ref[j], cols)
            weighted_all[j, :, cols] = weighted
            total = total + nt(weighted, scaled_all[j, :, cols])
        cross[j] = jnp.where(lower(), total, 0.0)

    @pl.when(step == 2 * nblocks - 1)
    def _():
        for copy in gathers("fsdp", nf, f, coef, (s2, r2)):
            copy.wait()

        def local_states(j, carry):
            short = coef[j].astype(jnp.bfloat16)
            write, read = short[:nstate], short[nstate:]
            for cols in pieces(channels):
                decay = base[BLK - 1 :, cols] * reach_ref[j, BLK - 1 :]
                state = pack[:nstate, cols]
                sofar = pack[size:, cols]
                term = factor * nn(read, weighted_all[j, :, cols])
                states[j, :, cols] = state
                before[j, :, cols] = sofar[:1]
                terms[j, :, cols] = term
                pack[:nstate, cols] = decay * state + decay * nn(write, scaled_all[j, :, cols])
                pack[nstate:size, cols] = pack[nstate:size, cols] + sofar[:1] * term
                pack[size:, cols] = sofar * decay
            return carry

        lax.fori_loop(0, nblocks, local_states, 0)
        for d in range(nc):
            packed[d] = pack[:, d * width : (d + 1) * width]
        out = [
            copy_to("ctx", nc, c, k, packed.at[lax.rem(c + k, nc)], arriving.at[c], (s3, r3))
            for k in range(1, nc)
        ]
        for copy in out:
            copy.start()
        arriving[c] = packed[c]
        for copy in out:
            copy.wait()
        state = jnp.zeros((nstate, width), jnp.float32)
        later = state
        for k in range(nc):
            leaving[k, :nstate] = state
            state = arriving[k, :nstate] + arriving[k, size : size + 1] * state
            j = nc - 1 - k
            leaving[j, nstate:] = later
            later = arriving[j, nstate:size] + arriving[j, size : size + 1] * later
        back = [
            copy_to("ctx", nc, c, k, leaving.at[lax.rem(c + k, nc)], home.at[c], (s4, r4))
            for k in range(1, nc)
        ]
        for copy in back:
            copy.start()
        home[c] = leaving[c]
        for copy in back:
            copy.wait()
        for d in range(nc):
            arrived[:, d * width : (d + 1) * width] = home[d]
        adjoint[...] = arrived[nstate:]
        exact = dict(precision=lax.Precision.HIGHEST)

        def local_grads(k, carry):
            j = nblocks - 1 - k
            write_part = jnp.zeros((nstate, BLK), jnp.float32)
            read_part = jnp.zeros((nstate, BLK), jnp.float32)
            for cols in pieces(channels):
                decay = base[BLK - 1 :, cols] * reach_ref[j, BLK - 1 :]
                later = decay * adjoint[:, cols]
                carried = later.astype(jnp.bfloat16)
                adjoint[:, cols] = terms[j, :, cols] + later
                carried_ref[j, :, cols] = carried
                state = states[j, :, cols] + before[j, :, cols] * arrived[:nstate, cols]
                write_part = write_part + nt(carried, scaled_all[j, :, cols])
                read_part = read_part + nt(state.astype(jnp.bfloat16), weighted_all[j, :, cols])
            wide = coef[j]
            gpart[j, :nstate] = factor * nn(wide[nstate:], cross[j], **exact) + write_part
            gpart[j, nstate:] = factor * (read_part + nt(wide[:nstate], cross[j], **exact))
            return carry

        lax.fori_loop(0, nblocks, local_grads, 0)
        for copy in scatters("fsdp", nf, f, gpart, ggot, (s5, r5)):
            copy.start()
        proj[...] = jnp.zeros_like(proj)
        summed("fsdp", nf, f, gpart, ggot, grad, (s5, r5))
        final = gathers("fsdp", nf, f, grad, (s6, r6))
        for copy in final:
            copy.start()
        for copy in final:
            copy.wait()

    @pl.when((step >= 2 * nblocks) & (step < 3 * nblocks))
    def _():
        full = grad[step - 2 * nblocks]
        high = full.astype(jnp.bfloat16)
        rest = full - high.astype(jnp.float32)
        middle = rest.astype(jnp.bfloat16)
        low = (rest - middle.astype(jnp.float32)).astype(jnp.bfloat16)
        stack = jnp.concatenate([high, middle, low], axis=0)
        for cols in pieces(channels):
            three = nn(stack, inner[:, cols])
            proj[:, cols] = proj[:, cols] + (
                three[:size] + (three[size : 2 * size] + three[2 * size :])
            )

    @pl.when(step == 3 * nblocks)
    def _():
        for d in range(nc):
            ppart[d] = proj[:, d * width : (d + 1) * width]
        for copy in scatters("ctx", nc, c, ppart, pgot, (s7, r7)):
            copy.start()

    @pl.when(step == 3 * nblocks + (5 * nblocks) // 8)
    def _():
        summed("ctx", nc, c, ppart, pgot, ptotal, (s7, r7))
        for copy in gathers("ctx", nc, c, ptotal, (s8, r8)):
            copy.start()

    @pl.when(step >= 3 * nblocks)
    def _():
        j = step - 3 * nblocks
        short = coef[j].astype(jnp.bfloat16)
        write, read = short[:nstate], short[nstate:]
        row = lax.broadcasted_iota(jnp.int32, (BLK, BLK), 0)
        col = lax.broadcasted_iota(jnp.int32, (BLK, BLK), 1)
        turned = jnp.where(col >= row, tn(write, read), 0.0).astype(jnp.bfloat16)
        high = grad[j].astype(jnp.bfloat16)
        recip = 1.0 / reach_ref[j]
        for cols in pieces(channels):
            mixed = factor * nn(turned, weighted_all[j, :, cols]) + tn(write, carried_ref[j, :, cols])
            value = inverse[:, cols] * recip * mixed
            value = value + skip[:, cols] * upstream[:, cols].astype(jnp.float32)
            value = value + tn(high, weight[:, cols])
            out[:, cols] = value.astype(jnp.bfloat16)

    @pl.when(step == 4 * nblocks - 1)
    def _():
        for copy in gathers("ctx", nc, c, ptotal, (s8, r8)):
            copy.wait()
        for d in range(nc):
            proj_out[:, d * width : (d + 1) * width] = ptotal[d] / (nblocks * BLK * nc)


def local(inner, proj_weight, rates, keep, skip, upstream):
    length, channels = inner.shape
    nstate = proj_weight.shape[0] // 2
    size = 2 * nstate
    nblocks = length // BLK
    f32 = jnp.float32
    factor = 1.0 / nstate**0.5
    scale = jnp.sqrt(-jnp.expm1(-2.0 * rates))[None]
    rates = rates[None]
    reach = jnp.cumprod(keep.reshape(nblocks, BLK), axis=1).reshape(length, 1)
    nf, nc = lax.axis_size("fsdp"), lax.axis_size("ctx")
    bf16 = jnp.bfloat16
    whole = pl.BlockSpec(memory_space=pltpu.VMEM)
    shape = jax.ShapeDtypeStruct
    tables = [pltpu.VMEM((BLK, channels), f32)] * 2
    coefs = (nblocks, size, BLK)
    got = pltpu.VMEM((nf - 1, nblocks // nf, size, BLK), f32)
    entry = (nblocks, nstate, channels)
    width = channels // nc
    scratch = (
        tables
        + [pltpu.VMEM((nblocks, BLK, channels), bf16)] * 2
        + [pltpu.VMEM((nblocks, BLK, BLK), f32)]
        + [pltpu.VMEM(coefs, f32), got, pltpu.VMEM(coefs, f32)] * 2
        + [pltpu.VMEM(entry, f32), pltpu.VMEM((nblocks, 1, channels), f32), pltpu.VMEM(entry, f32)]
        + [pltpu.VMEM((size + 8, channels), f32)]
        + [pltpu.VMEM((nc, size + 8, width), f32)] * 2
        + [pltpu.VMEM((nc, size, width), f32)] * 2
        + [pltpu.VMEM((size, channels), f32), pltpu.VMEM((nstate, channels), f32)]
        + [pltpu.VMEM(entry, bf16), pltpu.VMEM((size, channels), f32)]
        + [pltpu.VMEM((nc, size, width), f32)]
        + [pltpu.VMEM((nc - 1, 1, size, width), f32), pltpu.VMEM((nc, size, width), f32)]
        + [pltpu.SemaphoreType.DMA((nf - 1,))] * 4
        + [pltpu.SemaphoreType.DMA((nc - 1,))] * 4
        + [pltpu.SemaphoreType.DMA((nf - 1,))] * 4
        + [pltpu.SemaphoreType.DMA((nc - 1,))] * 4
    )
    last = nblocks - 1

    def inner_at(i):
        return (jnp.where(i < 2 * nblocks, jnp.minimum(i, last), jnp.minimum(i - 2 * nblocks, last)), 0)

    def upstream_at(i):
        first = jnp.clip(i - nblocks, 0, last)
        return (jnp.where(i < 2 * nblocks, first, jnp.maximum(i - 3 * nblocks, 0)), 0)

    return pl.pallas_call(
        functools.partial(main_kernel, nstate, factor, nblocks, nf, nc),
        grid=(4 * nblocks,),
        in_specs=[
            pl.BlockSpec((BLK, channels), inner_at),
            pl.BlockSpec((BLK, channels), upstream_at),
            whole, whole, whole, whole, whole,
        ],
        out_specs=[
            pl.BlockSpec((BLK, channels), lambda i: (jnp.maximum(i - 3 * nblocks, 0), 0)),
            whole,
        ],
        out_shape=[shape((length, channels), bf16), shape((size, channels), f32)],
        scratch_shapes=scratch,
        compiler_params=pltpu.CompilerParams(
            dimension_semantics=("arbitrary",),
            vmem_limit_bytes=56 * 2**20,
            collective_id=0,
            has_side_effects=True,
        ),
    )(
        inner, upstream, proj_weight, reach.reshape(nblocks, BLK, 1), rates, scale, skip[None]
    )


def solution(mesh):
    placed = (P("ctx", "fsdp"), P(None, "fsdp"), P("fsdp"), P("ctx"), P("fsdp"), P("ctx", "fsdp"))
    return jax.shard_map(
        local,
        mesh=mesh,
        in_specs=placed,
        out_specs=(P("ctx", "fsdp"), P(None, "fsdp")),
        check_vma=False,
    )
```

```python
import functools

import jax
import jax.numpy as jnp
from jax import lax
from jax.experimental import pallas as pl
from jax.experimental.pallas import tpu as pltpu
from jax.sharding import PartitionSpec as P

BLK = 256
MESH = pl.DeviceIdType.MESH


def nt(left, right, **how):
    return lax.dot_general(
        left, right, (((1,), (1,)), ((), ())), preferred_element_type=jnp.float32, **how
    )


def tn(left, right):
    return lax.dot_general(
        left, right, (((0,), (0,)), ((), ())), preferred_element_type=jnp.float32
    )


def nn(left, right, **how):
    return jnp.dot(left, right, preferred_element_type=jnp.float32, **how)


def fill(rates_ref, scale_ref, base, inverse):
    offsets = lax.broadcasted_iota(jnp.int32, base.shape, 0).astype(jnp.float32) + 1.0
    base[...] = jnp.exp(-offsets * rates_ref[...])
    inverse[...] = scale_ref[...] / base[...]


def pieces(channels):
    width = 512 if channels % 512 == 0 else channels
    return [slice(at, at + width) for at in range(0, channels, width)]


def scaled_of(inner_ref, inverse, reach, cols):
    return (inner_ref[:, cols].astype(jnp.float32) * inverse[:, cols] * (1.0 / reach)).astype(jnp.bfloat16)


def weighted_of(upstream_ref, base, reach, cols):
    return (upstream_ref[:, cols].astype(jnp.float32) * (base[:, cols] * reach)).astype(jnp.bfloat16)


def lower():
    row = lax.broadcasted_iota(jnp.int32, (BLK, BLK), 0)
    col = lax.broadcasted_iota(jnp.int32, (BLK, BLK), 1)
    return row >= col


def copy_to(axis, n, me, k, src, dst, sems):
    return pltpu.make_async_remote_copy(
        src_ref=src,
        dst_ref=dst,
        send_sem=sems[0].at[k - 1],
        recv_sem=sems[1].at[k - 1],
        device_id={axis: lax.rem(me + k, n)},
        device_id_type=MESH,
    )


def scatters(axis, n, me, part, got, sems):
    per = part.shape[0] // n
    return [
        copy_to(
            axis, n, me, k, part.at[pl.ds(lax.rem(me + k, n) * per, per)], got.at[k - 1], sems
        )
        for k in range(1, n)
    ]


def slice_to(n, me, owner, part, got, sems):
    per = part.shape[0] // n
    k = lax.rem(owner - me + n, n)
    return pltpu.make_async_remote_copy(
        src_ref=part.at[pl.ds(owner * per, per)],
        dst_ref=got.at[k - 1],
        send_sem=sems[0].at[k - 1],
        recv_sem=sems[1].at[k - 1],
        device_id={"fsdp": owner},
        device_id_type=MESH,
    )


def gathers(axis, n, me, total, sems):
    per = total.shape[0] // n
    own = total.at[pl.ds(me * per, per)]
    return [copy_to(axis, n, me, k, own, own, sems) for k in range(1, n)]


def summed(axis, n, me, part, got, total, sems):
    per = part.shape[0] // n
    acc = part[pl.ds(me * per, per)]
    for k, copy in enumerate(scatters(axis, n, me, part, got, sems)):
        copy.wait()
        acc = acc + got[k]
    total[pl.ds(me * per, per)] = acc


def main_kernel(
    nstate, factor, nblocks, nf, nc,
    inner, upstream, weight, reach_ref, rates, scale, skip,
    out, proj_out,
    base, inverse, scaled_all, weighted_all, cross, part, got, coef, gpart, ggot, grad,
    states, before, terms, pack, packed, arriving, leaving, home, arrived, adjoint,
    carried_ref, proj, ppart, pgot, ptotal,
    s1, r1, s2, r2, s3, r3, s4, r4, s5, r5, s6, r6, s7, r7, s8, r8,
):
    step = pl.program_id(0)
    size = 2 * nstate
    channels = inner.shape[1]
    width = channels // nc
    f = lax.axis_index("fsdp")
    c = lax.axis_index("ctx")
    barrier = pltpu.get_barrier_semaphore()

    @pl.when(step == 0)
    def _():
        for axis, n, me in (("fsdp", nf, f), ("ctx", nc, c)):
            for k in range(1, n):
                pl.semaphore_signal(
                    barrier, inc=1, device_id={axis: lax.rem(me + k, n)}, device_id_type=MESH
                )
        fill(rates, scale, base, inverse)
        pack[:size] = jnp.zeros_like(pack[:size])
        pack[size:] = jnp.ones_like(pack[size:])

    @pl.when(step < nblocks)
    def _():
        part[step] = nt(weight[...], inner[...])
        for cols in pieces(channels):
            scaled_all[step, :, cols] = scaled_of(inner, inverse, reach_ref[step], cols)

    @pl.when(step == nblocks - nf)
    def _():
        pl.semaphore_wait(barrier, nf + nc - 2)

    @pl.when((step >= nblocks - nf) & (step < nblocks) & (step - (nblocks - nf) != f))
    def _():
        slice_to(nf, f, step - (nblocks - nf), part, got, (s1, r1)).start()

    @pl.when(step == nblocks + (3 * nblocks) // 8)
    def _():
        summed("fsdp", nf, f, part, got, coef, (s1, r1))
        for copy in gathers("fsdp", nf, f, coef, (s2, r2)):
            copy.start()

    @pl.when((step >= nblocks) & (step < 2 * nblocks))
    def _():
        j = step - nblocks
        total = jnp.zeros((BLK, BLK), jnp.float32)
        for cols in pieces(channels):
            weighted = weighted_of(upstream, base, reach_ref[j], cols)
            weighted_all[j, :, cols] = weighted
            total = total + nt(weighted, scaled_all[j, :, cols])
        cross[j] = jnp.where(lower(), total, 0.0)

    @pl.when(step == 2 * nblocks - 1)
    def _():
        for copy in gathers("fsdp", nf, f, coef, (s2, r2)):
            copy.wait()

        def local_states(j, carry):
            short = coef[j].astype(jnp.bfloat16)
            write, read = short[:nstate], short[nstate:]
            for cols in pieces(channels):
                decay = base[BLK - 1 :, cols] * reach_ref[j, BLK - 1 :]
                state = pack[:nstate, cols]
                sofar = pack[size:, cols]
                term = factor * nn(read, weighted_all[j, :, cols])
                states[j, :, cols] = state
                before[j, :, cols] = sofar[:1]
                terms[j, :, cols] = term
                pack[:nstate, cols] = decay * state + decay * nn(write, scaled_all[j, :, cols])
                pack[nstate:size, cols] = pack[nstate:size, cols] + sofar[:1] * term
                pack[size:, cols] = sofar * decay
            return carry

        lax.fori_loop(0, nblocks, local_states, 0)
        for d in range(nc):
            packed[d] = pack[:, d * width : (d + 1) * width]
        out = [
            copy_to("ctx", nc, c, k, packed.at[lax.rem(c + k, nc)], arriving.at[c], (s3, r3))
            for k in range(1, nc)
        ]
        for copy in out:
            copy.start()
        arriving[c] = packed[c]
        exact = dict(precision=lax.Precision.HIGHEST)

        def local_products(j, carry):
            wide = coef[j]
            gpart[j, :nstate] = factor * nn(wide[nstate:], cross[j], **exact)
            gpart[j, nstate:] = factor * nt(wide[:nstate], cross[j], **exact)
            return carry

        lax.fori_loop(0, nblocks, local_products, 0)
        for copy in out:
            copy.wait()
        state = jnp.zeros((nstate, width), jnp.float32)
        later = state
        for k in range(nc):
            leaving[k, :nstate] = state
            state = arriving[k, :nstate] + arriving[k, size : size + 1] * state
            j = nc - 1 - k
            leaving[j, nstate:] = later
            later = arriving[j, nstate:size] + arriving[j, size : size + 1] * later
        back = [
            copy_to("ctx", nc, c, k, leaving.at[lax.rem(c + k, nc)], home.at[c], (s4, r4))
            for k in range(1, nc)
        ]
        for copy in back:
            copy.start()
        home[c] = leaving[c]
        for copy in back:
            copy.wait()
        for d in range(nc):
            arrived[:, d * width : (d + 1) * width] = home[d]
        adjoint[...] = arrived[nstate:]

        def local_grads(k, last):
            j = last - k
            write_part = jnp.zeros((nstate, BLK), jnp.float32)
            read_part = jnp.zeros((nstate, BLK), jnp.float32)
            for cols in pieces(channels):
                decay = base[BLK - 1 :, cols] * reach_ref[j, BLK - 1 :]
                later = decay * adjoint[:, cols]
                carried = later.astype(jnp.bfloat16)
                adjoint[:, cols] = terms[j, :, cols] + later
                carried_ref[j, :, cols] = carried
                state = states[j, :, cols] + before[j, :, cols] * arrived[:nstate, cols]
                write_part = write_part + nt(carried, scaled_all[j, :, cols])
                read_part = read_part + nt(state.astype(jnp.bfloat16), weighted_all[j, :, cols])
            gpart[j, :nstate] = gpart[j, :nstate] + write_part
            gpart[j, nstate:] = gpart[j, nstate:] + factor * read_part
            return last

        per = nblocks // nf
        for owner in reversed(range(nf)):
            lax.fori_loop(0, per, local_grads, (owner + 1) * per - 1)

            @pl.when(f != owner)
            def _(owner=owner):
                slice_to(nf, f, owner, gpart, ggot, (s5, r5)).start()

        proj[...] = jnp.zeros_like(proj)
        summed("fsdp", nf, f, gpart, ggot, grad, (s5, r5))
        final = gathers("fsdp", nf, f, grad, (s6, r6))
        for copy in final:
            copy.start()
        for copy in final:
            copy.wait()

    @pl.when((step >= 2 * nblocks) & (step < 3 * nblocks))
    def _():
        full = grad[step - 2 * nblocks]
        high = full.astype(jnp.bfloat16)
        rest = full - high.astype(jnp.float32)
        middle = rest.astype(jnp.bfloat16)
        low = (rest - middle.astype(jnp.float32)).astype(jnp.bfloat16)
        stack = jnp.concatenate([high, middle, low], axis=0)
        for cols in pieces(channels):
            three = nn(stack, inner[:, cols])
            proj[:, cols] = proj[:, cols] + (
                three[:size] + (three[size : 2 * size] + three[2 * size :])
            )

    @pl.when(step == 3 * nblocks)
    def _():
        for d in range(nc):
            ppart[d] = proj[:, d * width : (d + 1) * width]
        for copy in scatters("ctx", nc, c, ppart, pgot, (s7, r7)):
            copy.start()

    @pl.when(step == 3 * nblocks + (5 * nblocks) // 8)
    def _():
        summed("ctx", nc, c, ppart, pgot, ptotal, (s7, r7))
        for copy in gathers("ctx", nc, c, ptotal, (s8, r8)):
            copy.start()

    @pl.when(step >= 3 * nblocks)
    def _():
        j = step - 3 * nblocks
        short = coef[j].astype(jnp.bfloat16)
        write, read = short[:nstate], short[nstate:]
        row = lax.broadcasted_iota(jnp.int32, (BLK, BLK), 0)
        col = lax.broadcasted_iota(jnp.int32, (BLK, BLK), 1)
        turned = jnp.where(col >= row, tn(write, read), 0.0).astype(jnp.bfloat16)
        high = grad[j].astype(jnp.bfloat16)
        recip = 1.0 / reach_ref[j]
        for cols in pieces(channels):
            mixed = factor * nn(turned, weighted_all[j, :, cols]) + tn(write, carried_ref[j, :, cols])
            value = inverse[:, cols] * recip * mixed
            value = value + skip[:, cols] * upstream[:, cols].astype(jnp.float32)
            value = value + tn(high, weight[:, cols])
            out[:, cols] = value.astype(jnp.bfloat16)

    @pl.when(step == 4 * nblocks - 1)
    def _():
        for copy in gathers("ctx", nc, c, ptotal, (s8, r8)):
            copy.wait()
        for d in range(nc):
            proj_out[:, d * width : (d + 1) * width] = ptotal[d] / (nblocks * BLK * nc)


def place_kernel(source, target):
    target[...] = source[...]


def local(inner, proj_weight, rates, keep, skip, upstream):
    length, channels = inner.shape
    nstate = proj_weight.shape[0] // 2
    size = 2 * nstate
    nblocks = length // BLK
    f32 = jnp.float32
    factor = 1.0 / nstate**0.5
    scale = jnp.sqrt(-jnp.expm1(-2.0 * rates))[None]
    rates = rates[None]
    reach = jnp.cumprod(keep.reshape(nblocks, BLK), axis=1).reshape(length, 1)
    nf, nc = lax.axis_size("fsdp"), lax.axis_size("ctx")
    bf16 = jnp.bfloat16
    whole = pl.BlockSpec(memory_space=pltpu.VMEM)
    shape = jax.ShapeDtypeStruct
    tables = [pltpu.VMEM((BLK, channels), f32)] * 2
    coefs = (nblocks, size, BLK)
    got = pltpu.VMEM((nf - 1, nblocks // nf, size, BLK), f32)
    entry = (nblocks, nstate, channels)
    width = channels // nc
    scratch = (
        tables
        + [pltpu.VMEM((nblocks, BLK, channels), bf16)] * 2
        + [pltpu.VMEM((nblocks, BLK, BLK), f32)]
        + [pltpu.VMEM(coefs, f32), got, pltpu.VMEM(coefs, f32)] * 2
        + [pltpu.VMEM(entry, f32), pltpu.VMEM((nblocks, 1, channels), f32), pltpu.VMEM(entry, f32)]
        + [pltpu.VMEM((size + 8, channels), f32)]
        + [pltpu.VMEM((nc, size + 8, width), f32)] * 2
        + [pltpu.VMEM((nc, size, width), f32)] * 2
        + [pltpu.VMEM((size, channels), f32), pltpu.VMEM((nstate, channels), f32)]
        + [pltpu.VMEM(entry, bf16), pltpu.VMEM((size, channels), f32)]
        + [pltpu.VMEM((nc, size, width), f32)]
        + [pltpu.VMEM((nc - 1, 1, size, width), f32), pltpu.VMEM((nc, size, width), f32)]
        + [pltpu.SemaphoreType.DMA((nf - 1,))] * 4
        + [pltpu.SemaphoreType.DMA((nc - 1,))] * 4
        + [pltpu.SemaphoreType.DMA((nf - 1,))] * 4
        + [pltpu.SemaphoreType.DMA((nc - 1,))] * 4
    )
    last = nblocks - 1

    def inner_at(i):
        return (jnp.where(i < 2 * nblocks, jnp.minimum(i, last), jnp.minimum(i - 2 * nblocks, last)), 0)

    def upstream_at(i):
        first = jnp.clip(i - nblocks, 0, last)
        return (jnp.where(i < 2 * nblocks, first, jnp.maximum(i - 3 * nblocks, 0)), 0)

    input_grad, proj_grad = pl.pallas_call(
        functools.partial(main_kernel, nstate, factor, nblocks, nf, nc),
        grid=(4 * nblocks,),
        in_specs=[
            pl.BlockSpec((BLK, channels), inner_at),
            pl.BlockSpec((BLK, channels), upstream_at),
            whole, whole, whole, whole, whole,
        ],
        out_specs=[
            pl.BlockSpec((BLK, channels), lambda i: (jnp.maximum(i - 3 * nblocks, 0), 0)),
            whole,
        ],
        out_shape=[shape((length, channels), bf16), shape((size, channels), f32)],
        scratch_shapes=scratch,
        compiler_params=pltpu.CompilerParams(
            dimension_semantics=("arbitrary",),
            vmem_limit_bytes=56 * 2**20,
            collective_id=0,
            has_side_effects=True,
        ),
    )(
        inner, upstream, proj_weight, reach.reshape(nblocks, BLK, 1), rates, scale, skip[None]
    )
    rows = pl.BlockSpec((BLK, channels), lambda i: (i, 0))
    placed = pl.pallas_call(
        place_kernel,
        grid=(nblocks,),
        in_specs=[rows],
        out_specs=rows,
        out_shape=shape((length, channels), bf16),
        compiler_params=pltpu.CompilerParams(dimension_semantics=("arbitrary",)),
    )(input_grad)
    return (placed, proj_grad)


def solution(mesh):
    placed = (P("ctx", "fsdp"), P(None, "fsdp"), P("fsdp"), P("ctx"), P("fsdp"), P("ctx", "fsdp"))
    return jax.shard_map(
        local,
        mesh=mesh,
        in_specs=placed,
        out_specs=(P("ctx", "fsdp"), P(None, "fsdp")),
        check_vma=False,
    )
```

```python
import functools

import jax
import jax.numpy as jnp
from jax import lax
from jax.experimental import pallas as pl
from jax.experimental.pallas import tpu as pltpu
from jax.sharding import PartitionSpec as P

BLK = 256
MESH = pl.DeviceIdType.MESH


def nt(left, right, **how):
    return lax.dot_general(
        left, right, (((1,), (1,)), ((), ())), preferred_element_type=jnp.float32, **how
    )


def tn(left, right):
    return lax.dot_general(
        left, right, (((0,), (0,)), ((), ())), preferred_element_type=jnp.float32
    )


def nn(left, right, **how):
    return jnp.dot(left, right, preferred_element_type=jnp.float32, **how)


def fill(rates_ref, scale_ref, base, inverse):
    offsets = lax.broadcasted_iota(jnp.int32, base.shape, 0).astype(jnp.float32) + 1.0
    base[...] = jnp.exp(-offsets * rates_ref[...])
    inverse[...] = scale_ref[...] / base[...]


def pieces(channels):
    width = 512 if channels % 512 == 0 else channels
    return [slice(at, at + width) for at in range(0, channels, width)]


def scaled_of(inner_ref, inverse, reach, cols):
    return (inner_ref[:, cols].astype(jnp.float32) * inverse[:, cols] * (1.0 / reach)).astype(jnp.bfloat16)


def weighted_of(upstream_ref, base, reach, cols):
    return (upstream_ref[:, cols].astype(jnp.float32) * (base[:, cols] * reach)).astype(jnp.bfloat16)


def lower():
    row = lax.broadcasted_iota(jnp.int32, (BLK, BLK), 0)
    col = lax.broadcasted_iota(jnp.int32, (BLK, BLK), 1)
    return row >= col


def copy_to(axis, n, me, k, src, dst, sems):
    return pltpu.make_async_remote_copy(
        src_ref=src,
        dst_ref=dst,
        send_sem=sems[0].at[k - 1],
        recv_sem=sems[1].at[k - 1],
        device_id={axis: lax.rem(me + k, n)},
        device_id_type=MESH,
    )


def scatters(axis, n, me, part, got, sems):
    per = part.shape[0] // n
    return [
        copy_to(
            axis, n, me, k, part.at[pl.ds(lax.rem(me + k, n) * per, per)], got.at[k - 1], sems
        )
        for k in range(1, n)
    ]


def slice_to(n, me, owner, part, got, sems):
    per = part.shape[0] // n
    k = lax.rem(owner - me + n, n)
    return pltpu.make_async_remote_copy(
        src_ref=part.at[pl.ds(owner * per, per)],
        dst_ref=got.at[k - 1],
        send_sem=sems[0].at[k - 1],
        recv_sem=sems[1].at[k - 1],
        device_id={"fsdp": owner},
        device_id_type=MESH,
    )


def gathers(axis, n, me, total, sems):
    per = total.shape[0] // n
    own = total.at[pl.ds(me * per, per)]
    return [copy_to(axis, n, me, k, own, own, sems) for k in range(1, n)]


def summed(axis, n, me, part, got, total, sems):
    per = part.shape[0] // n
    acc = part[pl.ds(me * per, per)]
    for k, copy in enumerate(scatters(axis, n, me, part, got, sems)):
        copy.wait()
        acc = acc + got[k]
    total[pl.ds(me * per, per)] = acc


def main_kernel(
    nstate, factor, nblocks, nf, nc,
    inner, upstream, weight, reach_ref, rates, scale, skip,
    out, proj_out,
    base, inverse, scaled_all, weighted_all, cross, part, got, coef, gpart, ggot, grad,
    states, before, terms, pack, packed, arriving, leaving, home, arrived, adjoint,
    carried_ref, proj, ppart, pgot, ptotal,
    s1, r1, s2, r2, s3, r3, s4, r4, s5, r5, s6, r6, s7, r7, s8, r8,
):
    step = pl.program_id(0)
    size = 2 * nstate
    channels = inner.shape[1]
    width = channels // nc
    f = lax.axis_index("fsdp")
    c = lax.axis_index("ctx")
    barrier = pltpu.get_barrier_semaphore()

    @pl.when(step == 0)
    def _():
        for axis, n, me in (("fsdp", nf, f), ("ctx", nc, c)):
            for k in range(1, n):
                pl.semaphore_signal(
                    barrier, inc=1, device_id={axis: lax.rem(me + k, n)}, device_id_type=MESH
                )
        fill(rates, scale, base, inverse)
        pack[:size] = jnp.zeros_like(pack[:size])
        pack[size:] = jnp.ones_like(pack[size:])

    @pl.when(step < nblocks)
    def _():
        part[step] = nt(weight[...], inner[...])
        for cols in pieces(channels):
            scaled_all[step, :, cols] = scaled_of(inner, inverse, reach_ref[step], cols)

    @pl.when(step == nblocks - nf)
    def _():
        pl.semaphore_wait(barrier, nf + nc - 2)

    @pl.when((step >= nblocks - nf) & (step < nblocks) & (step - (nblocks - nf) != f))
    def _():
        slice_to(nf, f, step - (nblocks - nf), part, got, (s1, r1)).start()

    @pl.when(step == nblocks + (3 * nblocks) // 8)
    def _():
        summed("fsdp", nf, f, part, got, coef, (s1, r1))
        for copy in gathers("fsdp", nf, f, coef, (s2, r2)):
            copy.start()

    @pl.when((step >= nblocks) & (step < 2 * nblocks))
    def _():
        j = step - nblocks
        total = jnp.zeros((BLK, BLK), jnp.float32)
        for cols in pieces(channels):
            weighted = weighted_of(upstream, base, reach_ref[j], cols)
            weighted_all[j, :, cols] = weighted
            total = total + nt(weighted, scaled_all[j, :, cols])
        cross[j] = jnp.where(lower(), total, 0.0)

    @pl.when(step == 2 * nblocks - 1)
    def _():
        for copy in gathers("fsdp", nf, f, coef, (s2, r2)):
            copy.wait()

        def local_states(j, carry):
            short = coef[j].astype(jnp.bfloat16)
            write, read = short[:nstate], short[nstate:]
            for cols in pieces(channels):
                decay = base[BLK - 1 :, cols] * reach_ref[j, BLK - 1 :]
                state = pack[:nstate, cols]
                sofar = pack[size:, cols]
                term = factor * nn(read, weighted_all[j, :, cols])
                states[j, :, cols] = state
                before[j, :, cols] = sofar[:1]
                terms[j, :, cols] = term
                pack[:nstate, cols] = decay * state + decay * nn(write, scaled_all[j, :, cols])
                pack[nstate:size, cols] = pack[nstate:size, cols] + sofar[:1] * term
                pack[size:, cols] = sofar * decay
            return carry

        lax.fori_loop(0, nblocks, local_states, 0)
        for d in range(nc):
            packed[d] = pack[:, d * width : (d + 1) * width]
        out = [
            copy_to("ctx", nc, c, k, packed.at[lax.rem(c + k, nc)], arriving.at[c], (s3, r3))
            for k in range(1, nc)
        ]
        for copy in out:
            copy.start()
        arriving[c] = packed[c]
        exact = dict(precision=lax.Precision.HIGHEST)

        def local_products(j, carry):
            wide = coef[j]
            gpart[j, :nstate] = factor * nn(wide[nstate:], cross[j], **exact)
            gpart[j, nstate:] = factor * nt(wide[:nstate], cross[j], **exact)
            return carry

        lax.fori_loop(0, nblocks, local_products, 0)
        for copy in out:
            copy.wait()
        state = jnp.zeros((nstate, width), jnp.float32)
        later = state
        for k in range(nc):
            leaving[k, :nstate] = state
            state = arriving[k, :nstate] + arriving[k, size : size + 1] * state
            j = nc - 1 - k
            leaving[j, nstate:] = later
            later = arriving[j, nstate:size] + arriving[j, size : size + 1] * later
        back = [
            copy_to("ctx", nc, c, k, leaving.at[lax.rem(c + k, nc)], home.at[c], (s4, r4))
            for k in range(1, nc)
        ]
        for copy in back:
            copy.start()
        home[c] = leaving[c]
        for copy in back:
            copy.wait()
        for d in range(nc):
            arrived[:, d * width : (d + 1) * width] = home[d]
        adjoint[...] = arrived[nstate:]

        def local_grads(k, last):
            j = last - k
            write_part = jnp.zeros((nstate, BLK), jnp.float32)
            read_part = jnp.zeros((nstate, BLK), jnp.float32)
            for cols in pieces(channels):
                decay = base[BLK - 1 :, cols] * reach_ref[j, BLK - 1 :]
                later = decay * adjoint[:, cols]
                carried = later.astype(jnp.bfloat16)
                adjoint[:, cols] = terms[j, :, cols] + later
                carried_ref[j, :, cols] = carried
                state = states[j, :, cols] + before[j, :, cols] * arrived[:nstate, cols]
                write_part = write_part + nt(carried, scaled_all[j, :, cols])
                read_part = read_part + nt(state.astype(jnp.bfloat16), weighted_all[j, :, cols])
            gpart[j, :nstate] = gpart[j, :nstate] + write_part
            gpart[j, nstate:] = gpart[j, nstate:] + factor * read_part
            return last

        per = nblocks // nf
        for owner in reversed(range(nf)):
            lax.fori_loop(0, per, local_grads, (owner + 1) * per - 1)

            @pl.when(f != owner)
            def _(owner=owner):
                slice_to(nf, f, owner, gpart, ggot, (s5, r5)).start()

        proj[...] = jnp.zeros_like(proj)
        summed("fsdp", nf, f, gpart, ggot, grad, (s5, r5))
        final = gathers("fsdp", nf, f, grad, (s6, r6))
        for copy in final:
            copy.start()
        for copy in final:
            copy.wait()

    @pl.when((step >= 2 * nblocks) & (step < 3 * nblocks))
    def _():
        full = grad[step - 2 * nblocks]
        high = full.astype(jnp.bfloat16)
        rest = full - high.astype(jnp.float32)
        middle = rest.astype(jnp.bfloat16)
        low = (rest - middle.astype(jnp.float32)).astype(jnp.bfloat16)
        stack = jnp.concatenate([high, middle, low], axis=0)
        for cols in pieces(channels):
            three = nn(stack, inner[:, cols])
            proj[:, cols] = proj[:, cols] + (
                three[:size] + (three[size : 2 * size] + three[2 * size :])
            )

    @pl.when(step == 3 * nblocks)
    def _():
        for d in range(nc):
            ppart[d] = proj[:, d * width : (d + 1) * width]
        for copy in scatters("ctx", nc, c, ppart, pgot, (s7, r7)):
            copy.start()

    @pl.when(step == 3 * nblocks + (5 * nblocks) // 8)
    def _():
        summed("ctx", nc, c, ppart, pgot, ptotal, (s7, r7))
        for copy in gathers("ctx", nc, c, ptotal, (s8, r8)):
            copy.start()

    @pl.when(step >= 3 * nblocks)
    def _():
        j = step - 3 * nblocks
        short = coef[j].astype(jnp.bfloat16)
        write, read = short[:nstate], short[nstate:]
        row = lax.broadcasted_iota(jnp.int32, (BLK, BLK), 0)
        col = lax.broadcasted_iota(jnp.int32, (BLK, BLK), 1)
        turned = jnp.where(col >= row, tn(write, read), 0.0).astype(jnp.bfloat16)
        high = grad[j].astype(jnp.bfloat16)
        recip = 1.0 / reach_ref[j]
        for cols in pieces(channels):
            mixed = factor * nn(turned, weighted_all[j, :, cols]) + tn(write, carried_ref[j, :, cols])
            value = inverse[:, cols] * recip * mixed
            value = value + skip[:, cols] * upstream[:, cols].astype(jnp.float32)
            value = value + tn(high, weight[:, cols])
            out[pl.ds(j * BLK, BLK), cols] = value.astype(jnp.bfloat16)

    @pl.when(step == 4 * nblocks - 1)
    def _():
        for copy in gathers("ctx", nc, c, ptotal, (s8, r8)):
            copy.wait()
        for d in range(nc):
            proj_out[:, d * width : (d + 1) * width] = ptotal[d] / (nblocks * BLK * nc)


def place_kernel(source, target):
    target[...] = source[pl.ds(pl.program_id(0) * BLK, BLK), :]


def local(inner, proj_weight, rates, keep, skip, upstream):
    length, channels = inner.shape
    nstate = proj_weight.shape[0] // 2
    size = 2 * nstate
    nblocks = length // BLK
    f32 = jnp.float32
    factor = 1.0 / nstate**0.5
    scale = jnp.sqrt(-jnp.expm1(-2.0 * rates))[None]
    rates = rates[None]
    reach = jnp.cumprod(keep.reshape(nblocks, BLK), axis=1).reshape(length, 1)
    nf, nc = lax.axis_size("fsdp"), lax.axis_size("ctx")
    bf16 = jnp.bfloat16
    whole = pl.BlockSpec(memory_space=pltpu.VMEM)
    shape = jax.ShapeDtypeStruct
    tables = [pltpu.VMEM((BLK, channels), f32)] * 2
    coefs = (nblocks, size, BLK)
    got = pltpu.VMEM((nf - 1, nblocks // nf, size, BLK), f32)
    entry = (nblocks, nstate, channels)
    width = channels // nc
    scratch = (
        tables
        + [pltpu.VMEM((nblocks, BLK, channels), bf16)] * 2
        + [pltpu.VMEM((nblocks, BLK, BLK), f32)]
        + [pltpu.VMEM(coefs, f32), got, pltpu.VMEM(coefs, f32)] * 2
        + [pltpu.VMEM(entry, f32), pltpu.VMEM((nblocks, 1, channels), f32), pltpu.VMEM(entry, f32)]
        + [pltpu.VMEM((size + 8, channels), f32)]
        + [pltpu.VMEM((nc, size + 8, width), f32)] * 2
        + [pltpu.VMEM((nc, size, width), f32)] * 2
        + [pltpu.VMEM((size, channels), f32), pltpu.VMEM((nstate, channels), f32)]
        + [pltpu.VMEM(entry, bf16), pltpu.VMEM((size, channels), f32)]
        + [pltpu.VMEM((nc, size, width), f32)]
        + [pltpu.VMEM((nc - 1, 1, size, width), f32), pltpu.VMEM((nc, size, width), f32)]
        + [pltpu.SemaphoreType.DMA((nf - 1,))] * 4
        + [pltpu.SemaphoreType.DMA((nc - 1,))] * 4
        + [pltpu.SemaphoreType.DMA((nf - 1,))] * 4
        + [pltpu.SemaphoreType.DMA((nc - 1,))] * 4
    )
    last = nblocks - 1

    def inner_at(i):
        return (jnp.where(i < 2 * nblocks, jnp.minimum(i, last), jnp.minimum(i - 2 * nblocks, last)), 0)

    def upstream_at(i):
        first = jnp.clip(i - nblocks, 0, last)
        return (jnp.where(i < 2 * nblocks, first, jnp.maximum(i - 3 * nblocks, 0)), 0)

    input_grad, proj_grad = pl.pallas_call(
        functools.partial(main_kernel, nstate, factor, nblocks, nf, nc),
        grid=(4 * nblocks,),
        in_specs=[
            pl.BlockSpec((BLK, channels), inner_at),
            pl.BlockSpec((BLK, channels), upstream_at),
            whole, whole, whole, whole, whole,
        ],
        out_specs=[
            whole,
            whole,
        ],
        out_shape=[pltpu.VMEM((length, channels), bf16), shape((size, channels), f32)],
        scratch_shapes=scratch,
        compiler_params=pltpu.CompilerParams(
            dimension_semantics=("arbitrary",),
            vmem_limit_bytes=46 * 2**20,
            collective_id=0,
            has_side_effects=True,
        ),
    )(
        inner, upstream, proj_weight, reach.reshape(nblocks, BLK, 1), rates, scale, skip[None]
    )
    rows = pl.BlockSpec((BLK, channels), lambda i: (i, 0))
    placed = pl.pallas_call(
        place_kernel,
        grid=(nblocks,),
        in_specs=[whole],
        out_specs=rows,
        out_shape=shape((length, channels), bf16),
        compiler_params=pltpu.CompilerParams(
            dimension_semantics=("arbitrary",), vmem_limit_bytes=32 * 2**20
        ),
    )(input_grad)
    return (placed, proj_grad)


def solution(mesh):
    placed = (P("ctx", "fsdp"), P(None, "fsdp"), P("fsdp"), P("ctx"), P("fsdp"), P("ctx", "fsdp"))
    return jax.shard_map(
        local,
        mesh=mesh,
        in_specs=placed,
        out_specs=(P("ctx", "fsdp"), P(None, "fsdp")),
        check_vma=False,
    )
```
